128 devices in a mesh: tm: 8 (over x, z_lo), dp: 16 (over z_hi, y, core).
Axes of the slice: x: 4, y: 4, z: 4 (z_hi: 2, z_lo: 2; z = z_hi * 2 + z_lo), core: 2. Of those that a mesh axis runs over, the one named last changes fastest.
Arguments:
- clips: bfloat16 [16, 32, 32, 64, 128], P('dp', 'tm'), may hold values from -6 to 6
- weight: bfloat16 [3, 3, 3, 128, 256], replicated, may hold values from -0.109375 to 0.109375
- bias: float32 [256], replicated, may hold values from -3 to 3
- out_grad: bfloat16 [16, 16, 16, 32, 256], P('dp', 'tm'), may hold values from -6 to 6
Outputs:
- features: bfloat16 [16, 16, 16, 32, 256], P('dp', 'tm')
- clips_grad: bfloat16 [16, 32, 32, 64, 128], P('dp', 'tm')
- weight_grad: float32 [3, 3, 3, 128, 256], replicated
- bias_grad: float32 [256], replicated
The draws below stay inside these ranges and needn't reach their ends.
All inputs are finite; a program needn't handle non-finite values.
Results may differ from the reference program's by a relative error of at most 0.005.
Values may be sent and summed in bfloat16 or wider, within the bound.
No kernel may reach another device: no remote copies, remote signals or barrier semaphores. Data moves between devices by JAX's collectives and lax.ppermute only.
A program may use at most 64 MiB of HBM per device.

```python
import math
import jax
import jax.numpy as jnp
from jax import lax

C_IN = 128
C_OUT = 256
ROWS = 32
COLS = 64
BATCH = 16
FRAMES = 32
OUTPOS = 131072


def level_of(key, extent, shards, smallest, high):
    def one(axis_at, shards_of):
        steps = jax.random.uniform(jax.random.fold_in(jax.random.fold_in(key, 6), axis_at), (shards_of,), jnp.float32, smallest / len(shards), high / len(shards))
        return jnp.repeat(jnp.exp(steps), extent[axis_at] // shards_of).reshape((-1,) + (1,) * (len(extent) - axis_at - 1))

    factor_of = one(*shards[0])
    for cut in shards[1:]:
        factor_of = factor_of * one(*cut)
    return factor_of


def normal_values(own_key, shape, deviation, limit, cuts=(), held_as=jnp.bfloat16):
    level = level_of(own_key, shape, cuts, -0.22, 0.18) if cuts else 1.0
    values = jax.random.normal(own_key, shape, jnp.float32) * deviation * level
    return jnp.minimum(jnp.maximum(values, -limit), limit).astype(held_as)


def setup_inputs(seed: int = 0) -> dict:
    arg_keys = jax.random.split(jax.random.key(seed), 5)
    return {
        "clips": normal_values(arg_keys[0], (BATCH, FRAMES, ROWS, COLS, C_IN), 1.0, 6.0, ((0, 16), (1, 8))),
        "weight": normal_values(arg_keys[1], (3, 3, 3, C_IN, C_OUT), (27 * C_IN) ** -0.5, 0.109375),
        "bias": normal_values(arg_keys[2], (C_OUT,), 0.5, 3.0, (), jnp.float32),
        "out_grad": normal_values(arg_keys[3], (BATCH, FRAMES // 2, ROWS // 2, COLS // 2, C_OUT), 1.0, 6.0, ((0, 16), (1, 8))),
    }


def conv_forward(padded, kernel):
    return lax.conv_general_dilated(padded, kernel, (2, 2, 2), ((0, 0), (1, 1), (1, 1)), dimension_numbers=('NDHWC', 'DHWIO', 'NDHWC'), precision=lax.Precision.HIGHEST)

def reference(clips, weight, bias, out_grad):
    kernel = weight.astype(jnp.float32)

    def one_clip(pair):
        frames_in, grad_in = pair
        padded = jnp.pad(frames_in.astype(jnp.float32)[None], ((0, 0), (2, 0), (0, 0), (0, 0), (0, 0)))
        pre = conv_forward(padded, kernel)[0] + bias
        sig = jax.nn.sigmoid(pre)
        feats = (pre * sig).astype(jnp.bfloat16)
        pre_grad = (grad_in.astype(jnp.float32) * (sig * (1.0 + pre * (1.0 - sig)))).astype(jnp.bfloat16)
        _, pull = jax.vjp(conv_forward, padded, kernel)
        padded_grad, kernel_grad = pull(pre_grad.astype(jnp.float32)[None])
        input_grad = padded_grad[0, 2:].astype(jnp.bfloat16)
        bias_part = lax.optimization_barrier(jnp.sum(pre_grad.astype(jnp.float32), axis=(0, 1, 2)))
        return (feats, input_grad, kernel_grad, bias_part)
    feats, input_grad, kernel_grads, bias_parts = lax.map(one_clip, (clips, out_grad))
    scale = 1.0 / math.sqrt(OUTPOS)
    weight_grad = lax.optimization_barrier(jnp.sum(kernel_grads, axis=0)) * scale
    bias_grad = lax.optimization_barrier(jnp.sum(bias_parts, axis=0)) * scale
    return (feats, input_grad, weight_grad, bias_grad)
```

```python
import itertools
import math

import jax
import jax.numpy as jnp
from jax import lax
from jax.experimental import pallas as pl
from jax.experimental.pallas import tpu as pltpu
from jax.sharding import PartitionSpec as P

BF = jnp.bfloat16
F32 = jnp.float32
AXES = ("tm", "dp")
MIB = 1 << 20


def device_index(x, y, z, core):
    return (x * 2 + z % 2) * 16 + (z // 2) * 8 + y * 2 + core


PLACES = list(itertools.product(range(4), range(4), range(4), range(2)))
CORE_SWAP = [
    (device_index(x, y, z, c), device_index(x, y, z, 1 - c)) for x, y, z, c in PLACES
]
SAME_CORE = [[device_index(*q) for q in PLACES if q[3] == c] for c in range(2)]


def dot(a, b, ca, cb):
    return lax.dot_general(a, b, (((ca,), (cb,)), ((), ())), preferred_element_type=F32)


def patches_of(x_ref, frame, stage, p_ref, slot):
    zeros = jnp.zeros((8, 128), F32)
    for s in range(4):
        stage[s, 0:8, :] = zeros
    p_ref[slot, 0:32, 0:384] = jnp.zeros((32, 384), BF)

    def step(k, carry):
        for s in range(4):
            stage[s, 8:72, :] = x_ref[0, frame, 4 * k + s].astype(F32)
        for s in range(4):
            taps = [stage[s, pl.ds(7 + j, 32, stride=2), :].astype(BF) for j in range(3)]
            half = 2 * k + s // 2
            here = pl.ds(pl.multiple_of(half * 32, 32), 32)
            below = pl.ds(pl.multiple_of(half * 32 + 32, 32), 32)
            for j in range(3):
                if s % 2 == 0:
                    p_ref[slot, here, 384 + 128 * j : 512 + 128 * j] = taps[j]
                else:
                    p_ref[slot, here, 768 + 128 * j : 896 + 128 * j] = taps[j]
                    p_ref[slot, below, 128 * j : 128 * j + 128] = taps[j]
        return carry

    lax.fori_loop(0, 8, step, 0)


def head_kernel(x_ref, w_ref, p_ref, s_ref, stage):
    for slot in range(2):
        patches_of(x_ref, 2 + slot, stage, p_ref, slot)
    s_ref[...] = (
        dot(p_ref[0, 0:512], w_ref[0], 1, 0) + dot(p_ref[1, 0:512], w_ref[1], 1, 0)
    ).astype(BF)


def gate(pre, grad):
    sig = jax.nn.sigmoid(pre)
    return pre * sig, grad * (sig * (1.0 + pre * (1.0 - sig)))


def body_kernel(x_ref, w_ref, b_ref, g_ref, q_ref, p_ref, feat_ref, pg_ref, pre_ref, dw_ref, stage):
    for slot in range(2):
        patches_of(x_ref, slot, stage, p_ref, slot)
    bias = b_ref[...]
    pre = (
        dot(p_ref[0, 0:512], w_ref[0], 1, 0)
        + dot(p_ref[1, 0:512], w_ref[1], 1, 0)
        + dot(q_ref[0, 0:512], w_ref[2], 1, 0)
        + bias
    )
    feat, grad = gate(pre, g_ref[0, 1].reshape(512, 256).astype(F32))
    feat_ref[...] = feat.astype(BF)
    pg_ref[...] = grad.astype(BF)
    pre_ref[...] = dot(p_ref[0, 0:512], w_ref[2], 1, 0) + bias
    dw_ref[0] = dot(p_ref[0, 0:512], pg_ref[...], 0, 0)
    dw_ref[1] = dot(p_ref[1, 0:512], pg_ref[...], 0, 0)
    dw_ref[2] = dot(q_ref[0, 0:512], pg_ref[...], 0, 0)


def first_kernel(pre_ref, s_ref, g_ref, f1_ref, feat_ref, pg_ref):
    feat, grad = gate(pre_ref[...] + s_ref[...].astype(F32), g_ref[0, 0].reshape(512, 256).astype(F32))
    feat_ref[0, 0] = feat.astype(BF).reshape(16, 32, 256)
    feat_ref[0, 1] = f1_ref[...].reshape(16, 32, 256)
    pg_ref[...] = grad.astype(BF)


def middle_kernel(p_ref, pg0_ref, dw_ref, out_ref):
    out_ref[...] = dw_ref[2] + dot(p_ref[0, 0:512], pg0_ref[...], 0, 0)


def weight_kernel(core_ref, q_ref, pn_ref, pg0_ref, pg1_ref, dw_ref, dw2_ref, out_ref):
    core = core_ref[0]

    def put(rows, value):
        value = value.astype(BF)
        out_ref[core, rows, :] = value[:, 0:128]
        out_ref[1 - core, rows, :] = value[:, 128:256]

    put(slice(2304, 3456), dw2_ref[...])
    for kt in range(2):
        put(
            slice(1152 * kt, 1152 * kt + 1152),
            dw_ref[kt] + dot(q_ref[kt, 0:512], pn_ref[...], 0, 0),
        )
    total = jnp.sum(pg0_ref[...].astype(F32) + pg1_ref[...].astype(F32), axis=0, keepdims=True)
    put(slice(3456, 3584), jnp.broadcast_to(total, (128, 256)))


def back_kernel(w_ref, pg0_ref, pg1_ref, pn_ref, out_ref, pgs, even, odd, stage):
    last = lax.broadcasted_iota(jnp.int32, (512, 256), 0) % 32 == 31
    for k, ref in enumerate((pg0_ref, pg1_ref, pn_ref)):
        here = ref[...]
        pgs[k, 0, 0:512] = here
        moved = jnp.where(last, 0.0, pltpu.roll(here.astype(F32), 511, 0))
        pgs[k, 1, 0:512] = moved.astype(BF)
        pgs[k, 0, 512:544] = jnp.zeros((32, 256), BF)
        pgs[k, 1, 512:544] = jnp.zeros((32, 256), BF)
    sources = (((0, 2), (1, 0)), ((1, 1),), ((1, 2), (2, 0)), ((2, 1),))
    for frame, terms in enumerate(sources):
        for n, (k, kt) in enumerate(terms):
            def rows(kh, kw, count):
                start = 384 * kh + 128 * kw
                return w_ref[kt, start : start + 128 * count, :]

            e = dot(pgs[k, 0, 0:512], rows(1, 1, 2), 1, 1)
            o = dot(pgs[k, 0, 0:512], rows(2, 1, 2), 1, 1) + dot(pgs[k, 0, 32:544], rows(0, 1, 2), 1, 1)
            es = dot(pgs[k, 1, 0:512], rows(1, 0, 1), 1, 1)
            os = dot(pgs[k, 1, 0:512], rows(2, 0, 1), 1, 1) + dot(pgs[k, 1, 32:544], rows(0, 0, 1), 1, 1)
            if n == 0:
                even[...] = e
                odd[...] = o
            else:
                even[...] += e
                odd[...] += o
            even[:, 128:256] += es
            odd[:, 128:256] += os

        def step(h, carry):
            here = pl.ds(pl.multiple_of(h * 32, 32), 32)
            for s, acc in enumerate((even, odd)):
                stage[s, pl.ds(0, 32, stride=2), :] = acc[here, 0:128]
                stage[s, pl.ds(1, 32, stride=2), :] = acc[here, 128:256]
            for s in range(2):
                out_ref[0, frame, 2 * h + s] = stage[s, 0:64, :].astype(BF)
            return carry

        lax.fori_loop(0, 16, step, 0)


VM = pl.BlockSpec(memory_space=pltpu.VMEM)
SM = pl.BlockSpec(memory_space=pltpu.SMEM)


def call(kernel, name, outs, scratch, limit, flops, specs):
    moved = sum(math.prod(s) * d.dtype.itemsize for s, d in ((o.shape, o) for o in outs))
    return pl.pallas_call(
        kernel,
        name=name,
        out_shape=outs if len(outs) > 1 else outs[0],
        in_specs=specs,
        out_specs=[VM] * len(outs) if len(outs) > 1 else VM,
        scratch_shapes=scratch,
        compiler_params=pltpu.CompilerParams(vmem_limit_bytes=limit * MIB),
        cost_estimate=pl.CostEstimate(flops=flops, bytes_accessed=2 * moved, transcendentals=0),
    )


def shape(*dims, dtype=BF):
    return jax.ShapeDtypeStruct(dims, dtype)


def passed_along(value, steps):
    count = lax.axis_size("tm")
    first, last = (max(0, -steps), min(count, count - steps))
    return lax.ppermute(value, "tm", [(source, source + steps) for source in range(first, last)])


def local(clips, weight, bias, out_grad):
    w = weight.reshape(3, 1152, 256)
    unit = 2 * 512 * 1152 * 256
    stage = pltpu.VMEM((4, 72, 128), F32)
    q, part = call(
        head_kernel, "head", [shape(2, 544, 1152), shape(512, 256)], [stage], 8, 2 * unit, [VM] * 2
    )(clips, w)
    prior = passed_along(part, 1)
    p, feat1, pg1, pre0, dw = call(
        body_kernel,
        "body",
        [
            shape(2, 544, 1152),
            shape(512, 256),
            shape(512, 256),
            shape(512, 256, dtype=F32),
            shape(3, 1152, 256, dtype=F32),
        ],
        [stage],
        16,
        7 * unit,
        [VM] * 5,
    )(clips, w, bias.reshape(1, 256), out_grad, q)
    features, pg0 = call(
        first_kernel, "first", [shape(1, 2, 16, 32, 256), shape(512, 256)], [], 8, unit // 10, [VM] * 4
    )(pre0, prior, out_grad, feat1)
    after = passed_along(pg0, -1)
    dw2 = call(middle_kernel, "middle", [shape(1152, 256, dtype=F32)], [], 8, unit, [VM] * 3)(p, pg0, dw)
    core = (lax.axis_index("dp") % 2).astype(jnp.int32).reshape(1)
    halves = call(
        weight_kernel, "weight", [shape(2, 3584, 128)], [], 8, 2 * unit, [SM] + [VM] * 6
    )(core, q, after, pg0, pg1, dw, dw2)
    got = lax.ppermute(halves[1], AXES, CORE_SWAP)
    mine = (halves[0].astype(F32) + got.astype(F32)).astype(BF)
    spread = lax.all_to_all(
        mine.reshape(64, 56, 128), AXES, split_axis=0, concat_axis=0, tiled=True, axis_index_groups=SAME_CORE
    )
    clips_grad = call(
        back_kernel,
        "back",
        [shape(1, 4, 32, 64, 128)],
        [
            pltpu.VMEM((3, 2, 544, 256), BF),
            pltpu.VMEM((512, 256), F32),
            pltpu.VMEM((512, 256), F32),
            pltpu.VMEM((2, 64, 128), F32),
        ],
        16,
        8 * unit,
        [VM] * 4,
    )(w, pg0, pg1, after)
    scale = 1.0 / math.sqrt(1024 * lax.axis_size("tm") * lax.axis_size("dp"))
    own = (jnp.sum(spread.astype(F32), axis=0) * scale).astype(BF)
    whole = lax.all_to_all(
        jnp.broadcast_to(own[None], (64, 56, 128)),
        AXES,
        split_axis=0,
        concat_axis=0,
        tiled=True,
        axis_index_groups=SAME_CORE,
    ).reshape(3584, 128)
    other = lax.ppermute(whole, AXES, CORE_SWAP)
    low = jnp.where(core[0] == 0, whole, other)
    high = jnp.where(core[0] == 0, other, whole)
    sums = jnp.concatenate([low, high], axis=1).astype(F32)
    return features, clips_grad, sums[:3456].reshape(3, 3, 3, 128, 256), sums[3456]


def solution(mesh):
    in_specs = (P("dp", "tm", None, None, None), P(), P(), P("dp", "tm", None, None, None))
    out_specs = (P("dp", "tm", None, None, None), P("dp", "tm", None, None, None), P(), P())
    return jax.shard_map(local, mesh=mesh, in_specs=in_specs, out_specs=out_specs, check_vma=False)
```

```python
import itertools
import math

import jax
import jax.numpy as jnp
from jax import lax
from jax.experimental import pallas as pl
from jax.experimental.pallas import tpu as pltpu
from jax.sharding import PartitionSpec as P


BF = jnp.bfloat16
F32 = jnp.float32
AXES = ("tm", "dp")
MIB = 1 << 20


def device_index(x, y, z, core):
    return (x * 2 + z % 2) * 16 + (z // 2) * 8 + y * 2 + core


PLACES = list(itertools.product(range(4), range(4), range(4), range(2)))
CORE_SWAP = [
    (device_index(x, y, z, c), device_index(x, y, z, 1 - c)) for x, y, z, c in PLACES
]
RING = (3, 2, 1, 0)
ROW_SWAP = [(device_index(x, y, z, c), device_index(x, RING[y], z, c)) for x, y, z, c in PLACES]
TEAMS = [
    [device_index(x, y, z, c) for x in range(4) for y in pair for z in range(4)]
    for pair in ((0, 1), (3, 2))
    for c in range(2)
]
TEAM = len(TEAMS[0])
SHARE = 3584 // TEAM


def dot(a, b, ca, cb):
    return lax.dot_general(a, b, (((ca,), (cb,)), ((), ())), preferred_element_type=F32)


def patches_of(x_ref, frame, stage, p_ref, slot):
    zeros = jnp.zeros((8, 128), F32)
    for s in range(4):
        stage[s, 0:8, :] = zeros
    p_ref[slot, 0:32, 0:384] = jnp.zeros((32, 384), BF)

    def step(k, carry):
        for s in range(4):
            stage[s, 8:72, :] = x_ref[0, frame, 4 * k + s].astype(F32)
        for s in range(4):
            taps = [stage[s, pl.ds(7 + j, 32, stride=2), :].astype(BF) for j in range(3)]
            half = 2 * k + s // 2
            here = pl.ds(pl.multiple_of(half * 32, 32), 32)
            below = pl.ds(pl.multiple_of(half * 32 + 32, 32), 32)
            for j in range(3):
                if s % 2 == 0:
                    p_ref[slot, here, 384 + 128 * j : 512 + 128 * j] = taps[j]
                else:
                    p_ref[slot, here, 768 + 128 * j : 896 + 128 * j] = taps[j]
                    p_ref[slot, below, 128 * j : 128 * j + 128] = taps[j]
        return carry

    lax.fori_loop(0, 8, step, 0)


def head_kernel(x_ref, w_ref, s_ref, x, w, stage, patches, sems):
    copies = []
    for n, frame in enumerate((2, 3, 0, 1)):
        copies.append(pltpu.make_async_copy(x_ref.at[0, frame], x.at[0, frame], sems.at[n]))
    for kt in range(3):
        copies.append(pltpu.make_async_copy(w_ref.at[kt], w.at[kt], sems.at[4 + kt]))
    for n in (0, 4, 1, 5, 2, 3, 6):
        copies[n].start()
    for slot in range(2):
        copies[slot].wait()
        patches_of(x, 2 + slot, stage, patches, slot)
    for slot in range(2):
        copies[4 + slot].wait()
    s_ref[...] = (
        dot(patches[0, 0:512], w[0], 1, 0) + dot(patches[1, 0:512], w[1], 1, 0)
    ).astype(BF)
    for n in (2, 3, 6):
        copies[n].wait()


def gate(pre, grad):
    sig = jax.nn.sigmoid(pre)
    return pre * sig, grad * (sig * (1.0 + pre * (1.0 - sig)))


def body_kernel(x_ref, w_ref, b_ref, g_ref, feat_ref, pg_ref, pre_ref, stage, patches):
    for slot in range(3):
        patches_of(x_ref, slot, stage, patches, slot)
    bias = b_ref[...]
    pre_ref[...] = dot(patches[0, 0:512], w_ref[2], 1, 0) + bias
    pre = bias
    for slot in range(3):
        pre = pre + dot(patches[slot, 0:512], w_ref[slot], 1, 0)
    feat, grad = gate(pre, g_ref[0, 1].reshape(512, 256).astype(F32))
    feat_ref[...] = feat.astype(BF)
    pg_ref[...] = grad.astype(BF)


def first_kernel(pre_ref, s_ref, g_ref, f1_ref, feat_ref, pg_ref):
    feat, grad = gate(pre_ref[...] + s_ref[...].astype(F32), g_ref[0, 0].reshape(512, 256).astype(F32))
    feat_ref[0, 0] = feat.astype(BF).reshape(16, 32, 256)
    feat_ref[0, 1] = f1_ref[...].reshape(16, 32, 256)
    pg_ref[...] = grad.astype(BF)


def middle_kernel(x_ref, pg0_ref, pg1_ref, q_ref, dw_ref, stage, patches):
    for slot in range(2):
        patches_of(x_ref, slot, stage, patches, slot)
        patches_of(x_ref, 2 + slot, stage, q_ref, slot)
    dw_ref[0] = dot(patches[0, 0:512], pg1_ref[...], 0, 0)
    dw_ref[1] = dot(patches[1, 0:512], pg1_ref[...], 0, 0)
    dw_ref[2] = dot(q_ref[0, 0:512], pg1_ref[...], 0, 0) + dot(patches[0, 0:512], pg0_ref[...], 0, 0)


def weight_kernel(core_ref, q_ref, pn_ref, pg0_ref, pg1_ref, dw_ref, out_ref):
    core = core_ref[0]

    def put(rows, value):
        value = value.astype(BF)
        out_ref[core, rows, :] = value[:, 0:128]
        out_ref[1 - core, rows, :] = value[:, 128:256]

    put(slice(2304, 3456), dw_ref[2])
    for kt in range(2):
        put(
            slice(1152 * kt, 1152 * kt + 1152),
            dw_ref[kt] + dot(q_ref[kt, 0:512], pn_ref[...], 0, 0),
        )
    total = jnp.sum(pg0_ref[...].astype(F32) + pg1_ref[...].astype(F32), axis=0, keepdims=True)
    put(slice(3456, 3584), jnp.broadcast_to(total, (128, 256)))


def put_half(half, src_ref, out_ref, wide, sems):
    copies = []
    for n in range(4):
        rows = slice(864 * n, 864 * n + 864)
        wide[rows, :] = src_ref[rows, :].astype(F32)
        there = out_ref.at[pl.ds(864 * n, 864), pl.ds(pl.multiple_of(half * 128, 128), 128)]
        copies.append(pltpu.make_async_copy(wide.at[rows, :], there, sems.at[n]))
        copies[n].start()
    for copy in copies:
        copy.wait()


def own_kernel(core_ref, own_ref, out_ref, wide, sems):
    put_half(core_ref[0], own_ref, out_ref, wide, sems)


def other_kernel(core_ref, own_ref, other_ref, held_ref, out_ref, bias_ref, wide, sems):
    own = own_ref[3456:3464, :].astype(F32)[0:1]
    other = other_ref[3456:3464, :].astype(F32)[0:1]
    first = core_ref[0] == 0
    bias_ref[:, 0:128] = jnp.where(first, own, other)
    bias_ref[:, 128:256] = jnp.where(first, other, own)
    put_half(1 - core_ref[0], other_ref, out_ref, wide, sems)


def back_kernel(w_ref, pg0_ref, pg1_ref, pn_ref, out_ref, pgs, even, odd, stage):
    last = lax.broadcasted_iota(jnp.int32, (512, 256), 0) % 32 == 31
    for k, ref in enumerate((pg0_ref, pg1_ref, pn_ref)):
        here = ref[...]
        pgs[k, 0, 0:512] = here
        moved = jnp.where(last, 0.0, pltpu.roll(here.astype(F32), 511, 0))
        pgs[k, 1, 0:512] = moved.astype(BF)
        pgs[k, 0, 512:544] = jnp.zeros((32, 256), BF)
        pgs[k, 1, 512:544] = jnp.zeros((32, 256), BF)
    sources = (((0, 2), (1, 0)), ((1, 1),), ((1, 2), (2, 0)), ((2, 1),))
    for frame, terms in enumerate(sources):
        for n, (k, kt) in enumerate(terms):
            def rows(kh, kw, count):
                start = 384 * kh + 128 * kw
                return w_ref[kt, start : start + 128 * count, :]

            e = dot(pgs[k, 0, 0:512], rows(1, 1, 2), 1, 1)
            o = dot(pgs[k, 0, 0:512], rows(2, 1, 2), 1, 1) + dot(pgs[k, 0, 32:544], rows(0, 1, 2), 1, 1)
            es = dot(pgs[k, 1, 0:512], rows(1, 0, 1), 1, 1)
            os = dot(pgs[k, 1, 0:512], rows(2, 0, 1), 1, 1) + dot(pgs[k, 1, 32:544], rows(0, 0, 1), 1, 1)
            if n == 0:
                even[...] = e
                odd[...] = o
            else:
                even[...] += e
                odd[...] += o
            even[:, 128:256] += es
            odd[:, 128:256] += os

        def step(h, carry):
            here = pl.ds(pl.multiple_of(h * 32, 32), 32)
            for s, acc in enumerate((even, odd)):
                stage[s, pl.ds(0, 32, stride=2), :] = acc[here, 0:128]
                stage[s, pl.ds(1, 32, stride=2), :] = acc[here, 128:256]
            for s in range(2):
                out_ref[0, frame, 2 * h + s] = stage[s, 0:64, :].astype(BF)
            return carry

        lax.fori_loop(0, 16, step, 0)


VM = pl.BlockSpec(memory_space=pltpu.VMEM)
HB = pl.BlockSpec(memory_space=pltpu.HBM)
SM = pl.BlockSpec(memory_space=pltpu.SMEM)


def call(kernel, outs, scratch, limit, flops, specs):
    moved = sum(math.prod(s) * d.dtype.itemsize for s, d in ((o.shape, o) for o in outs))
    return pl.pallas_call(
        kernel,
        out_shape=outs if len(outs) > 1 else outs[0],
        in_specs=specs,
        out_specs=[VM] * len(outs) if len(outs) > 1 else VM,
        scratch_shapes=scratch,
        compiler_params=pltpu.CompilerParams(vmem_limit_bytes=limit * MIB),
        cost_estimate=pl.CostEstimate(flops=flops, bytes_accessed=2 * moved, transcendentals=0),
    )


def shape(*dims, dtype=BF):
    return jax.ShapeDtypeStruct(dims, dtype)


def in_hbm(value):
    return pltpu.with_memory_space_constraint(value, pltpu.HBM)


def passed_along(value, steps):
    count = lax.axis_size("tm")
    first, last = (max(0, -steps), min(count, count - steps))
    return lax.ppermute(value, "tm", [(source, source + steps) for source in range(first, last)])


def spread_over(value):
    return lax.all_to_all(
        value, AXES, split_axis=0, concat_axis=0, tiled=True, axis_index_groups=TEAMS
    )


def finish(core, own, other):
    params = pltpu.CompilerParams(vmem_limit_bytes=8 * MIB)
    cost = pl.CostEstimate(flops=1 << 20, bytes_accessed=3 * MIB, transcendentals=0)
    scratch = [pltpu.VMEM((3456, 128), F32), pltpu.SemaphoreType.DMA((4,))]
    held = pl.pallas_call(
        own_kernel,
        name="own",
        out_shape=shape(3456, 256, dtype=F32),
        in_specs=[SM, VM],
        out_specs=HB,
        scratch_shapes=scratch,
        compiler_params=params,
        cost_estimate=cost,
    )(core, own)
    return pl.pallas_call(
        other_kernel,
        name="other",
        out_shape=[shape(3456, 256, dtype=F32), shape(1, 256, dtype=F32)],
        in_specs=[SM, VM, VM, HB],
        out_specs=[HB, VM],
        scratch_shapes=scratch,
        input_output_aliases={3: 0},
        compiler_params=params,
        cost_estimate=cost,
    )(core, own, other, held)


def local(clips, weight, bias, out_grad):
    unit = 2 * 512 * 1152 * 256
    stage = pltpu.VMEM((4, 72, 128), F32)
    part, x, w = call(
        head_kernel,
        [pltpu.VMEM((512, 256), BF), pltpu.VMEM((1, 4, 32, 64, 128), BF), pltpu.VMEM((3, 1152, 256), BF)],
        [stage, pltpu.VMEM((2, 544, 1152), BF), pltpu.SemaphoreType.DMA((7,))],
        16,
        2 * unit,
        [HB] * 2,
    )(in_hbm(clips), in_hbm(weight.reshape(3, 1152, 256)))
    prior = passed_along(part, 1)
    feat1, pg1, pre0 = call(
        body_kernel,
        [shape(512, 256), shape(512, 256), shape(512, 256, dtype=F32)],
        [stage, pltpu.VMEM((3, 544, 1152), BF)],
        16,
        4 * unit,
        [VM] * 4,
    )(x, w, bias.reshape(1, 256), out_grad)
    features, pg0 = call(
        first_kernel, [shape(1, 2, 16, 32, 256), shape(512, 256)], [], 8, unit // 10, [VM] * 4
    )(pre0, prior, out_grad, feat1)
    after = passed_along(pg0, -1)
    q, dw = call(
        middle_kernel,
        [shape(2, 544, 1152), shape(3, 1152, 256, dtype=F32)],
        [stage, pltpu.VMEM((2, 544, 1152), BF)],
        16,
        4 * unit,
        [VM] * 3,
    )(x, pg0, pg1)
    core = (lax.axis_index("dp") % 2).astype(jnp.int32).reshape(1)
    halves = call(weight_kernel, [shape(2, 3584, 128)], [], 8, 2 * unit, [SM] + [VM] * 5)(core, q, after, pg0, pg1, dw)
    got = lax.ppermute(halves[1], AXES, CORE_SWAP)
    mine = (halves[0].astype(F32) + got.astype(F32)).astype(BF)
    pieces = spread_over(mine.reshape(TEAM, SHARE, 128))
    clips_grad = call(
        back_kernel,
        [shape(1, 4, 32, 64, 128)],
        [
            pltpu.VMEM((3, 2, 544, 256), BF),
            pltpu.VMEM((512, 256), F32),
            pltpu.VMEM((512, 256), F32),
            pltpu.VMEM((2, 64, 128), F32),
        ],
        16,
        8 * unit,
        [VM] * 4,
    )(w, pg0, pg1, after)
    positions = 1024 * lax.axis_size("tm") * lax.axis_size("dp")
    total = jnp.sum(pieces.astype(F32), axis=0)
    total = total + lax.ppermute(total, AXES, ROW_SWAP)
    total = (total * (1.0 / math.sqrt(positions))).astype(BF)
    own = spread_over(jnp.broadcast_to(total[None], (TEAM, SHARE, 128))).reshape(3584, 128)
    other = lax.ppermute(own, AXES, CORE_SWAP)
    weight_grad, bias_grad = finish(core, own, other)
    return features, clips_grad, weight_grad.reshape(3, 3, 3, 128, 256), bias_grad.reshape(256)


def solution(mesh):
    in_specs = (P("dp", "tm", None, None, None), P(), P(), P("dp", "tm", None, None, None))
    out_specs = (P("dp", "tm", None, None, None), P("dp", "tm", None, None, None), P(), P())
    return jax.shard_map(local, mesh=mesh, in_specs=in_specs, out_specs=out_specs, check_vma=False)
```

```python
import itertools
import math

import jax
import jax.numpy as jnp
from jax import lax
from jax.experimental import pallas as pl
from jax.experimental.pallas import tpu as pltpu
from jax.sharding import PartitionSpec as P


BF = jnp.bfloat16
F32 = jnp.float32
AXES = ("tm", "dp")
MIB = 1 << 20


def device_index(x, y, z, core):
    return (x * 2 + z % 2) * 16 + (z // 2) * 8 + y * 2 + core


PLACES = list(itertools.product(range(4), range(4), range(4), range(2)))
CORE_SWAP = [
    (device_index(x, y, z, c), device_index(x, y, z, 1 - c)) for x, y, z, c in PLACES
]
RING = (3, 2, 1, 0)
ROW_SWAP = [(device_index(x, y, z, c), device_index(x, RING[y], z, c)) for x, y, z, c in PLACES]
TEAMS = [
    [device_index(x, y, z, c) for x in (3, 2, 1, 0) for y in pair for z in (3, 2, 1, 0)]
    for pair in ((0, 1), (3, 2))
    for c in range(2)
]
TEAM = len(TEAMS[0])
SHARE = 3584 // TEAM


def dot(a, b, ca, cb):
    return lax.dot_general(a, b, (((ca,), (cb,)), ((), ())), preferred_element_type=F32)


def patches_of(x_ref, frame, stage, p_ref, slot):
    zeros = jnp.zeros((8, 128), F32)
    for s in range(4):
        stage[s, 0:8, :] = zeros
    p_ref[slot, 0:32, 0:384] = jnp.zeros((32, 384), BF)

    def step(k, carry):
        for s in range(4):
            stage[s, 8:72, :] = x_ref[0, frame, 4 * k + s].astype(F32)
        for s in range(4):
            taps = [stage[s, pl.ds(7 + j, 32, stride=2), :].astype(BF) for j in range(3)]
            half = 2 * k + s // 2
            here = pl.ds(pl.multiple_of(half * 32, 32), 32)
            below = pl.ds(pl.multiple_of(half * 32 + 32, 32), 32)
            for j in range(3):
                if s % 2 == 0:
                    p_ref[slot, here, 384 + 128 * j : 512 + 128 * j] = taps[j]
                else:
                    p_ref[slot, here, 768 + 128 * j : 896 + 128 * j] = taps[j]
                    p_ref[slot, below, 128 * j : 128 * j + 128] = taps[j]
        return carry

    lax.fori_loop(0, 8, step, 0)


def head_kernel(x_ref, w_ref, s_ref, x, w, stage, patches, sems):
    copies = [pltpu.make_async_copy(x_ref.at[0, frame], x.at[0, frame], sems.at[frame]) for frame in range(4)]
    copies += [pltpu.make_async_copy(w_ref.at[kt], w.at[kt], sems.at[4 + kt]) for kt in range(2)]
    for n in (2, 4, 3, 5, 0, 1):
        copies[n].start()
    for slot in range(2):
        copies[2 + slot].wait()
        patches_of(x, 2 + slot, stage, patches, slot)
    for slot in range(2):
        copies[4 + slot].wait()
    s_ref[...] = (
        dot(patches[0, 0:512], w[0], 1, 0) + dot(patches[1, 0:512], w[1], 1, 0)
    ).astype(BF)
    for n in range(2):
        copies[n].wait()


def gate(pre, grad):
    sig = jax.nn.sigmoid(pre)
    return pre * sig, grad * (sig * (1.0 + pre * (1.0 - sig)))


def body_kernel(
    x_ref, w_ref, b_ref, g_ref, feat_ref, pg_ref, pre_ref, out_ref, stage, patches, w, w_sems, *scratch
):
    loads = [pltpu.make_async_copy(w_ref.at[kt], w.at[kt], w_sems.at[kt]) for kt in range(3)]
    for load in loads:
        load.start()
    for slot in range(3):
        patches_of(x_ref, slot, stage, patches, slot)
    for load in loads:
        load.wait()
    bias = b_ref[...]
    pre_ref[...] = dot(patches[0, 0:512], w[2], 1, 0) + bias
    pre = bias
    for slot in range(3):
        pre = pre + dot(patches[slot, 0:512], w[slot], 1, 0)
    feat, grad = gate(pre, g_ref[0, 1].reshape(512, 256).astype(F32))
    feat_ref[...] = feat.astype(BF)
    pg_ref[...] = grad.astype(BF)
    back_body(w, (pg_ref,), 1, (((0, 1),),), out_ref, *scratch)


def first_kernel(pre_ref, s_ref, g_ref, feat_ref, pg_ref):
    feat, grad = gate(pre_ref[...] + s_ref[...].astype(F32), g_ref[0, 0].reshape(512, 256).astype(F32))
    feat_ref[...] = feat.astype(BF)
    pg_ref[...] = grad.astype(BF)


def put(core, out_ref, rows, value):
    value = value.astype(BF)
    out_ref[core, rows, :] = value[:, 0:128]
    out_ref[1 - core, rows, :] = value[:, 128:256]


def middle_kernel(
    core_ref,
    x_ref,
    w_ref,
    pg0_ref,
    pg1_ref,
    f0_ref,
    f1_ref,
    held_ref,
    feat_ref,
    q_ref,
    dw_ref,
    out_ref,
    grad_ref,
    stage,
    patches,
    w,
    own_sems,
    *scratch,
):
    copies = [
        pltpu.make_async_copy(ref, feat_ref.at[n], own_sems.at[n]) for n, ref in enumerate((f0_ref, f1_ref))
    ]
    loads = [pltpu.make_async_copy(w_ref.at[kt], w.at[kt], own_sems.at[2 + kt]) for kt in range(3)]
    for copy in loads + copies:
        copy.start()
    for slot in range(2):
        patches_of(x_ref, slot, stage, patches, slot)
        patches_of(x_ref, 2 + slot, stage, q_ref, slot)
    put(
        core_ref[0],
        out_ref,
        slice(0, 1152),
        dot(q_ref[0, 0:512], pg1_ref[...], 0, 0) + dot(patches[0, 0:512], pg0_ref[...], 0, 0),
    )
    total = jnp.sum(pg0_ref[...].astype(F32) + pg1_ref[...].astype(F32), axis=0, keepdims=True)
    put(core_ref[0], out_ref, slice(1152, 1280), jnp.broadcast_to(total, (128, 256)))
    dw_ref[0] = dot(patches[0, 0:512], pg1_ref[...], 0, 0)
    dw_ref[1] = dot(patches[1, 0:512], pg1_ref[...], 0, 0)
    for copy in loads:
        copy.wait()
    back_body(w, (pg0_ref, pg1_ref), 0, (((0, 2), (1, 0)),), grad_ref, *scratch)
    for copy in copies:
        copy.wait()


def weight_kernel(core_ref, q_ref, pn_ref, dw_ref, out_ref):
    for kt in range(2):
        put(
            core_ref[0],
            out_ref,
            slice(1152 * kt, 1152 * kt + 1152),
            dw_ref[kt] + dot(q_ref[kt, 0:512], pn_ref[...], 0, 0),
        )


def join_kernel(late_ref, late_got_ref, early_ref, early_got_ref, out_ref):
    for rows, kept, got in (
        (slice(0, 2304), late_ref, late_got_ref),
        (slice(2304, 3584), early_ref, early_got_ref),
    ):
        out_ref[rows, :] = (kept[0].astype(F32) + got[...].astype(F32)).astype(BF)


def put_half(half, src_ref, out_ref, wide, sems):
    copies = []
    for n in range(4):
        rows = slice(864 * n, 864 * n + 864)
        wide[rows, :] = src_ref[rows, :].astype(F32)
        there = out_ref.at[pl.ds(864 * n, 864), pl.ds(pl.multiple_of(half * 128, 128), 128)]
        copies.append(pltpu.make_async_copy(wide.at[rows, :], there, sems.at[n]))
        copies[n].start()
    return copies


def own_kernel(core_ref, own_ref, out_ref, wide, sems):
    for copy in put_half(core_ref[0], own_ref, out_ref, wide, sems):
        copy.wait()


def other_kernel(core_ref, own_ref, other_ref, held_ref, out_ref, bias_ref, wide, line, sems):
    own = own_ref[3456:3464, :].astype(F32)[0:1]
    other = other_ref[3456:3464, :].astype(F32)[0:1]
    first = core_ref[0] == 0
    line[:, 0:128] = jnp.where(first, own, other)
    line[:, 128:256] = jnp.where(first, other, own)
    bias_copy = pltpu.make_async_copy(line, bias_ref, sems.at[4])
    bias_copy.start()
    for copy in put_half(1 - core_ref[0], other_ref, out_ref, wide, sems):
        copy.wait()
    bias_copy.wait()


def back_body(w_ref, refs, first, sources, out_ref, pgs, even, odd, stage, held, sems):
    last = lax.broadcasted_iota(jnp.int32, (512, 256), 0) % 32 == 31
    for k, ref in enumerate(refs):
        here = ref[...]
        pgs[k, 0, 0:512] = here
        moved = jnp.where(last, 0.0, pltpu.roll(here.astype(F32), 511, 0))
        pgs[k, 1, 0:512] = moved.astype(BF)
        pgs[k, 0, 512:544] = jnp.zeros((32, 256), BF)
        pgs[k, 1, 512:544] = jnp.zeros((32, 256), BF)
    copies = []
    for frame, terms in enumerate(sources):
        for n, (k, kt) in enumerate(terms):
            def rows(kh, kw, count):
                start = 384 * kh + 128 * kw
                return w_ref[kt, start : start + 128 * count, :]

            e = dot(pgs[k, 0, 0:512], rows(1, 1, 2), 1, 1)
            o = dot(pgs[k, 0, 0:512], rows(2, 1, 2), 1, 1) + dot(pgs[k, 0, 32:544], rows(0, 1, 2), 1, 1)
            es = dot(pgs[k, 1, 0:512], rows(1, 0, 1), 1, 1)
            os = dot(pgs[k, 1, 0:512], rows(2, 0, 1), 1, 1) + dot(pgs[k, 1, 32:544], rows(0, 0, 1), 1, 1)
            if n == 0:
                even[...] = e
                odd[...] = o
            else:
                even[...] += e
                odd[...] += o
            even[:, 128:256] += es
            odd[:, 128:256] += os

        def step(h, carry):
            here = pl.ds(pl.multiple_of(h * 32, 32), 32)
            for s, acc in enumerate((even, odd)):
                stage[s, pl.ds(0, 32, stride=2), :] = acc[here, 0:128]
                stage[s, pl.ds(1, 32, stride=2), :] = acc[here, 128:256]
            for s in range(2):
                held[frame, 2 * h + s] = stage[s, 0:64, :].astype(BF)
            return carry

        lax.fori_loop(0, 16, step, 0)
        copies.append(pltpu.make_async_copy(held.at[frame], out_ref.at[0, first + frame], sems.at[frame]))
        copies[frame].start()
    for copy in copies:
        copy.wait()


def high_kernel(w_ref, pg1_ref, pn_ref, held_ref, out_ref, *scratch):
    back_body(w_ref, (pg1_ref, pn_ref), 2, (((0, 2), (1, 0)), ((1, 1),)), out_ref, *scratch)


JOINED = jax.ShapeDtypeStruct
VM = pl.BlockSpec(memory_space=pltpu.VMEM)
HB = pl.BlockSpec(memory_space=pltpu.HBM)
SM = pl.BlockSpec(memory_space=pltpu.SMEM)


def call(kernel, outs, scratch, limit, flops, specs, out_specs=None, aliases=None):
    moved = sum(math.prod(o.shape) * jnp.dtype(o.dtype).itemsize for o in outs)
    out_specs = out_specs or [VM] * len(outs)
    return pl.pallas_call(
        kernel,
        out_shape=outs if len(outs) > 1 else outs[0],
        in_specs=specs,
        out_specs=out_specs if len(outs) > 1 else out_specs[0],
        scratch_shapes=scratch,
        input_output_aliases=aliases or {},
        compiler_params=pltpu.CompilerParams(vmem_limit_bytes=limit * MIB),
        cost_estimate=pl.CostEstimate(flops=flops, bytes_accessed=2 * moved, transcendentals=0),
    )


def shape(*dims, dtype=BF):
    return jax.ShapeDtypeStruct(dims, dtype)


def in_hbm(value):
    return pltpu.with_memory_space_constraint(value, pltpu.HBM)


def passed_along(value, steps):
    count = lax.axis_size("tm")
    first, last = (max(0, -steps), min(count, count - steps))
    return lax.ppermute(value, "tm", [(source, source + steps) for source in range(first, last)])


def spread_over(value):
    return lax.all_to_all(
        value, AXES, split_axis=0, concat_axis=0, tiled=True, axis_index_groups=TEAMS
    )


def finish(core, own):
    other = lax.ppermute(own, AXES, CORE_SWAP)
    whole = shape(3456, 256, dtype=F32)
    wide = pltpu.VMEM((3456, 128), F32)
    held = call(own_kernel, [whole], [wide, pltpu.SemaphoreType.DMA((4,))], 8, 1 << 20, [SM, VM], [HB])(core, own)
    return call(
        other_kernel,
        [whole, shape(1, 256, dtype=F32)],
        [wide, pltpu.VMEM((1, 256), F32), pltpu.SemaphoreType.DMA((5,))],
        8,
        1 << 20,
        [SM, VM, VM, HB],
        [HB, HB],
        {3: 0},
    )(core, own, other, held)


def local(clips, weight, bias, out_grad):
    taps = weight.reshape(3, 1152, 256)
    unit = 2 * 512 * 1152 * 256
    stage = pltpu.VMEM((4, 72, 128), F32)
    part, x = call(
        head_kernel,
        [pltpu.VMEM((512, 256), BF), pltpu.VMEM((1, 4, 32, 64, 128), BF)],
        [pltpu.VMEM((2, 1152, 256), BF), stage, pltpu.VMEM((2, 544, 1152), BF), pltpu.SemaphoreType.DMA((6,))],
        16,
        2 * unit,
        [HB] * 2,
    )(in_hbm(clips), in_hbm(taps))
    prior = passed_along(part, 1)

    def grad_scratch(frames):
        return [
            pltpu.VMEM((2, 2, 544, 256), BF),
            pltpu.VMEM((512, 256), F32),
            pltpu.VMEM((512, 256), F32),
            pltpu.VMEM((2, 64, 128), F32),
            pltpu.VMEM((frames, 32, 64, 128), BF),
            pltpu.SemaphoreType.DMA((frames,)),
        ]

    grad_shape = shape(1, 4, 32, 64, 128)
    feat1, pg1, pre0, held = call(
        body_kernel,
        [
            pltpu.VMEM((512, 256), BF),
            pltpu.VMEM((512, 256), BF),
            pltpu.VMEM((512, 256), F32),
            grad_shape,
        ],
        [
            stage,
            pltpu.VMEM((3, 544, 1152), BF),
            pltpu.VMEM((3, 1152, 256), BF),
            pltpu.SemaphoreType.DMA((3,)),
        ]
        + grad_scratch(1),
        16,
        5 * unit,
        [VM, HB, VM, VM],
        [VM] * 3 + [HB],
    )(x, in_hbm(taps), bias.reshape(1, 256), out_grad)
    feat0, pg0 = call(
        first_kernel, [pltpu.VMEM((512, 256), BF), pltpu.VMEM((512, 256), BF)], [], 8, unit // 10, [VM] * 3
    )(pre0, prior, out_grad)
    after = passed_along(pg0, -1)
    core = (lax.axis_index("dp") % 2).astype(jnp.int32).reshape(1)
    features, q, dw, early, held = call(
        middle_kernel,
        [
            shape(2, 512, 256),
            pltpu.VMEM((2, 544, 1152), BF),
            pltpu.VMEM((2, 1152, 256), F32),
            pltpu.VMEM((2, 1280, 128), BF),
            grad_shape,
        ],
        [
            stage,
            pltpu.VMEM((2, 544, 1152), BF),
            pltpu.VMEM((3, 1152, 256), BF),
            pltpu.SemaphoreType.DMA((5,)),
        ]
        + grad_scratch(1),
        16,
        6 * unit,
        [SM, VM, HB] + [VM] * 4 + [HB],
        [HB, VM, VM, VM, HB],
        {7: 4},
    )(core, x, in_hbm(taps), pg0, pg1, feat0, feat1, held)
    early_got = lax.ppermute(early[1], AXES, CORE_SWAP)
    late = call(weight_kernel, [pltpu.VMEM((2, 2304, 128), BF)], [], 8, 2 * unit, [SM] + [VM] * 3)(core, q, after, dw)
    late_got = lax.ppermute(late[1], AXES, CORE_SWAP)
    mine = call(join_kernel, [JOINED((3584, 128), BF)], [], 8, unit // 10, [VM] * 4)(late, late_got, early, early_got)
    pieces = spread_over(mine.reshape(TEAM, SHARE, 128))
    clips_grad = call(
        high_kernel, [grad_shape], grad_scratch(2), 8, 4 * unit, [VM] * 3 + [HB], [HB], {3: 0}
    )(taps, pg1, after, held)
    positions = 1024 * lax.axis_size("tm") * lax.axis_size("dp")
    total = jnp.sum(pieces.astype(F32), axis=0)
    total = total + lax.ppermute(total, AXES, ROW_SWAP)
    total = (total * (1.0 / math.sqrt(positions))).astype(BF)
    own = spread_over(jnp.broadcast_to(total[None], (TEAM, SHARE, 128))).reshape(3584, 128)
    weight_grad, bias_grad = finish(core, own)
    features = features.reshape(1, 2, 16, 32, 256)
    return features, clips_grad, weight_grad.reshape(3, 3, 3, 128, 256), bias_grad.reshape(256)


def solution(mesh):
    in_specs = (P("dp", "tm", None, None, None), P(), P(), P("dp", "tm", None, None, None))
    out_specs = (P("dp", "tm", None, None, None), P("dp", "tm", None, None, None), P(), P())
    return jax.shard_map(local, mesh=mesh, in_specs=in_specs, out_specs=out_specs, check_vma=False)
```

```python
import itertools
import math

import jax
import jax.numpy as jnp
from jax import lax
from jax.experimental import pallas as pl
from jax.experimental.pallas import tpu as pltpu
from jax.sharding import PartitionSpec as P


BF = jnp.bfloat16
F32 = jnp.float32
AXES = ("tm", "dp")
MIB = 1 << 20


def device_index(x, y, z, core):
    return (x * 2 + z % 2) * 16 + (z // 2) * 8 + y * 2 + core


PLACES = list(itertools.product(range(4), range(4), range(4), range(2)))
CORE_SWAP = [
    (device_index(x, y, z, c), device_index(x, y, z, 1 - c)) for x, y, z, c in PLACES
]
RING = (3, 2, 1, 0)
ROW_SWAP = [(device_index(x, y, z, c), device_index(x, RING[y], z, c)) for x, y, z, c in PLACES]
TEAMS = [
    [device_index(x, y, z, c) for x in (3, 2, 1, 0) for y in pair for z in (3, 2, 1, 0)]
    for pair in ((0, 1), (3, 2))
    for c in range(2)
]
TEAM = len(TEAMS[0])
SHARE = 3584 // TEAM


def dot(a, b, ca, cb):
    return lax.dot_general(a, b, (((ca,), (cb,)), ((), ())), preferred_element_type=F32)


def patches_of(x_ref, frame, stage, p_ref, slot):
    zeros = jnp.zeros((8, 128), F32)
    for s in range(4):
        stage[s, 0:8, :] = zeros
    p_ref[slot, 0:32, 0:384] = jnp.zeros((32, 384), BF)

    def step(k, carry):
        for s in range(4):
            stage[s, 8:72, :] = x_ref[0, frame, 4 * k + s].astype(F32)
        for s in range(4):
            taps = [stage[s, pl.ds(7 + j, 32, stride=2), :].astype(BF) for j in range(3)]
            half = 2 * k + s // 2
            here = pl.ds(pl.multiple_of(half * 32, 32), 32)
            below = pl.ds(pl.multiple_of(half * 32 + 32, 32), 32)
            for j in range(3):
                if s % 2 == 0:
                    p_ref[slot, here, 384 + 128 * j : 512 + 128 * j] = taps[j]
                else:
                    p_ref[slot, here, 768 + 128 * j : 896 + 128 * j] = taps[j]
                    p_ref[slot, below, 128 * j : 128 * j + 128] = taps[j]
        return carry

    lax.fori_loop(0, 8, step, 0)


def head_kernel(x_ref, w_ref, s_ref, x, w, stage, patches, sems):
    copies = [pltpu.make_async_copy(x_ref.at[0, frame], x.at[0, frame], sems.at[frame]) for frame in range(4)]
    copies += [pltpu.make_async_copy(w_ref.at[kt], w.at[kt], sems.at[4 + kt]) for kt in range(2)]
    for n in (2, 3, 4, 5):
        copies[n].start()
    for slot in range(2):
        copies[2 + slot].wait()
        patches_of(x, 2 + slot, stage, patches, slot)
    for n in range(2):
        copies[n].start()
    for slot in range(2):
        copies[4 + slot].wait()
    s_ref[...] = (
        dot(patches[0, 0:512], w[0], 1, 0) + dot(patches[1, 0:512], w[1], 1, 0)
    ).astype(BF)
    for n in range(2):
        copies[n].wait()


def gate(pre, grad):
    sig = jax.nn.sigmoid(pre)
    return pre * sig, grad * (sig * (1.0 + pre * (1.0 - sig)))


def body_kernel(
    x_ref, w_ref, b_ref, g_ref, feat_ref, pg_ref, pre_ref, out_ref, stage, patches, w, w_sems, *scratch
):
    loads = [pltpu.make_async_copy(w_ref.at[kt], w.at[kt], w_sems.at[kt]) for kt in range(3)]
    for load in loads:
        load.start()
    for slot in range(3):
        patches_of(x_ref, slot, stage, patches, slot)
    for load in loads:
        load.wait()
    bias = b_ref[...]
    pre_ref[...] = dot(patches[0, 0:512], w[2], 1, 0) + bias
    pre = bias
    for slot in range(3):
        pre = pre + dot(patches[slot, 0:512], w[slot], 1, 0)
    feat, grad = gate(pre, g_ref[0, 1].reshape(512, 256).astype(F32))
    feat_ref[...] = feat.astype(BF)
    pg_ref[...] = grad.astype(BF)
    back_body(w, (pg_ref,), 1, (((0, 1),),), out_ref, *scratch)


def first_kernel(pre_ref, s_ref, g_ref, feat_ref, pg_ref):
    feat, grad = gate(pre_ref[...] + s_ref[...].astype(F32), g_ref[0, 0].reshape(512, 256).astype(F32))
    feat_ref[...] = feat.astype(BF)
    pg_ref[...] = grad.astype(BF)


def put(core, out_ref, rows, value):
    value = value.astype(BF)
    out_ref[core, rows, :] = value[:, 0:128]
    out_ref[1 - core, rows, :] = value[:, 128:256]


def middle_kernel(
    core_ref,
    x_ref,
    w_ref,
    pg0_ref,
    pg1_ref,
    f0_ref,
    f1_ref,
    held_ref,
    feat_ref,
    q_ref,
    dw_ref,
    out_ref,
    grad_ref,
    stage,
    patches,
    w,
    own_sems,
    *scratch,
):
    copies = [
        pltpu.make_async_copy(ref, feat_ref.at[n], own_sems.at[n]) for n, ref in enumerate((f0_ref, f1_ref))
    ]
    loads = [pltpu.make_async_copy(w_ref.at[kt], w.at[kt], own_sems.at[2 + kt]) for kt in (2, 0)]
    for copy in loads + copies:
        copy.start()
    for slot in range(2):
        patches_of(x_ref, slot, stage, patches, slot)
        patches_of(x_ref, 2 + slot, stage, q_ref, slot)
    put(
        core_ref[0],
        out_ref,
        slice(0, 1152),
        dot(q_ref[0, 0:512], pg1_ref[...], 0, 0) + dot(patches[0, 0:512], pg0_ref[...], 0, 0),
    )
    total = jnp.sum(pg0_ref[...].astype(F32) + pg1_ref[...].astype(F32), axis=0, keepdims=True)
    put(core_ref[0], out_ref, slice(1152, 1280), jnp.broadcast_to(total, (128, 256)))
    dw_ref[0] = dot(patches[0, 0:512], pg1_ref[...], 0, 0)
    dw_ref[1] = dot(patches[1, 0:512], pg1_ref[...], 0, 0)
    for copy in loads:
        copy.wait()
    back_body(w, (pg0_ref, pg1_ref), 0, (((0, 2), (1, 0)),), grad_ref, *scratch)
    for copy in copies:
        copy.wait()


def weight_kernel(core_ref, q_ref, pn_ref, dw_ref, out_ref):
    for kt in range(2):
        put(
            core_ref[0],
            out_ref,
            slice(1152 * kt, 1152 * kt + 1152),
            dw_ref[kt] + dot(q_ref[kt, 0:512], pn_ref[...], 0, 0),
        )


def join_kernel(late_ref, late_got_ref, early_ref, early_got_ref, out_ref):
    for rows, kept, got in (
        (slice(0, 2304), late_ref, late_got_ref),
        (slice(2304, 3584), early_ref, early_got_ref),
    ):
        out_ref[rows, :] = (kept[0].astype(F32) + got[...].astype(F32)).astype(BF)


def put_half(half, src_ref, out_ref, wide, sems):
    copies = []
    for n in range(4):
        rows = slice(864 * n, 864 * n + 864)
        wide[rows, :] = src_ref[rows, :].astype(F32)
        there = out_ref.at[pl.ds(864 * n, 864), pl.ds(pl.multiple_of(half * 128, 128), 128)]
        copies.append(pltpu.make_async_copy(wide.at[rows, :], there, sems.at[n]))
        copies[n].start()
    return copies


def own_kernel(core_ref, own_ref, out_ref, wide, sems):
    for copy in put_half(core_ref[0], own_ref, out_ref, wide, sems):
        copy.wait()


def other_kernel(core_ref, own_ref, other_ref, held_ref, out_ref, bias_ref, wide, line, sems):
    own = own_ref[3456:3464, :].astype(F32)[0:1]
    other = other_ref[3456:3464, :].astype(F32)[0:1]
    first = core_ref[0] == 0
    line[:, 0:128] = jnp.where(first, own, other)
    line[:, 128:256] = jnp.where(first, other, own)
    bias_copy = pltpu.make_async_copy(line, bias_ref, sems.at[4])
    bias_copy.start()
    for copy in put_half(1 - core_ref[0], other_ref, out_ref, wide, sems):
        copy.wait()
    bias_copy.wait()


def back_body(w_ref, refs, first, sources, out_ref, pgs, even, odd, stage, held, sems):
    last = lax.broadcasted_iota(jnp.int32, (512, 256), 0) % 32 == 31
    for k, ref in enumerate(refs):
        here = ref[...]
        pgs[k, 0, 0:512] = here
        moved = jnp.where(last, 0.0, pltpu.roll(here.astype(F32), 511, 0))
        pgs[k, 1, 0:512] = moved.astype(BF)
        pgs[k, 0, 512:544] = jnp.zeros((32, 256), BF)
        pgs[k, 1, 512:544] = jnp.zeros((32, 256), BF)
    copies = []
    for frame, terms in enumerate(sources):
        for n, (k, kt) in enumerate(terms):
            def rows(kh, kw, count):
                start = 384 * kh + 128 * kw
                return w_ref[kt, start : start + 128 * count, :]

            e = dot(pgs[k, 0, 0:512], rows(1, 1, 2), 1, 1)
            o = dot(pgs[k, 0, 0:512], rows(2, 1, 2), 1, 1) + dot(pgs[k, 0, 32:544], rows(0, 1, 2), 1, 1)
            es = dot(pgs[k, 1, 0:512], rows(1, 0, 1), 1, 1)
            os = dot(pgs[k, 1, 0:512], rows(2, 0, 1), 1, 1) + dot(pgs[k, 1, 32:544], rows(0, 0, 1), 1, 1)
            if n == 0:
                even[...] = e
                odd[...] = o
            else:
                even[...] += e
                odd[...] += o
            even[:, 128:256] += es
            odd[:, 128:256] += os

        def step(h, carry):
            here = pl.ds(pl.multiple_of(h * 32, 32), 32)
            for s, acc in enumerate((even, odd)):
                stage[s, pl.ds(0, 32, stride=2), :] = acc[here, 0:128]
                stage[s, pl.ds(1, 32, stride=2), :] = acc[here, 128:256]
            for s in range(2):
                held[frame, 2 * h + s] = stage[s, 0:64, :].astype(BF)
            return carry

        lax.fori_loop(0, 16, step, 0)
        copies.append(pltpu.make_async_copy(held.at[frame], out_ref.at[0, first + frame], sems.at[frame]))
        copies[frame].start()
    for copy in copies:
        copy.wait()


def high_kernel(w_ref, pg1_ref, pn_ref, held_ref, out_ref, *scratch):
    back_body(w_ref, (pg1_ref, pn_ref), 2, (((0, 2), (1, 0)), ((1, 1),)), out_ref, *scratch)


JOINED = jax.ShapeDtypeStruct
VM = pl.BlockSpec(memory_space=pltpu.VMEM)
HB = pl.BlockSpec(memory_space=pltpu.HBM)
SM = pl.BlockSpec(memory_space=pltpu.SMEM)


def call(kernel, outs, scratch, limit, flops, specs, out_specs=None, aliases=None):
    moved = sum(math.prod(o.shape) * jnp.dtype(o.dtype).itemsize for o in outs)
    out_specs = out_specs or [VM] * len(outs)
    return pl.pallas_call(
        kernel,
        out_shape=outs if len(outs) > 1 else outs[0],
        in_specs=specs,
        out_specs=out_specs if len(outs) > 1 else out_specs[0],
        scratch_shapes=scratch,
        input_output_aliases=aliases or {},
        compiler_params=pltpu.CompilerParams(vmem_limit_bytes=limit * MIB),
        cost_estimate=pl.CostEstimate(flops=flops, bytes_accessed=2 * moved, transcendentals=0),
    )


def shape(*dims, dtype=BF):
    return jax.ShapeDtypeStruct(dims, dtype)


def in_hbm(value):
    return pltpu.with_memory_space_constraint(value, pltpu.HBM)


def passed_along(value, steps):
    count = lax.axis_size("tm")
    first, last = (max(0, -steps), min(count, count - steps))
    return lax.ppermute(value, "tm", [(source, source + steps) for source in range(first, last)])


def spread_over(value):
    return lax.all_to_all(
        value, AXES, split_axis=0, concat_axis=0, tiled=True, axis_index_groups=TEAMS
    )


def finish(core, own):
    other = lax.ppermute(own, AXES, CORE_SWAP)
    whole = shape(3456, 256, dtype=F32)
    wide = pltpu.VMEM((3456, 128), F32)
    held = call(own_kernel, [whole], [wide, pltpu.SemaphoreType.DMA((4,))], 8, 1 << 20, [SM, VM], [HB])(core, own)
    return call(
        other_kernel,
        [whole, shape(1, 256, dtype=F32)],
        [wide, pltpu.VMEM((1, 256), F32), pltpu.SemaphoreType.DMA((5,))],
        8,
        1 << 20,
        [SM, VM, VM, HB],
        [HB, HB],
        {3: 0},
    )(core, own, other, held)


def local(clips, weight, bias, out_grad):
    taps = weight.reshape(3, 1152, 256)
    unit = 2 * 512 * 1152 * 256
    stage = pltpu.VMEM((4, 72, 128), F32)
    part, x = call(
        head_kernel,
        [pltpu.VMEM((512, 256), BF), pltpu.VMEM((1, 4, 32, 64, 128), BF)],
        [pltpu.VMEM((2, 1152, 256), BF), stage, pltpu.VMEM((2, 544, 1152), BF), pltpu.SemaphoreType.DMA((6,))],
        16,
        2 * unit,
        [HB] * 2,
    )(in_hbm(clips), in_hbm(taps))
    prior = passed_along(part, 1)

    def grad_scratch(frames):
        return [
            pltpu.VMEM((2, 2, 544, 256), BF),
            pltpu.VMEM((512, 256), F32),
            pltpu.VMEM((512, 256), F32),
            pltpu.VMEM((2, 64, 128), F32),
            pltpu.VMEM((frames, 32, 64, 128), BF),
            pltpu.SemaphoreType.DMA((frames,)),
        ]

    grad_shape = shape(1, 4, 32, 64, 128)
    feat1, pg1, pre0, held = call(
        body_kernel,
        [
            pltpu.VMEM((512, 256), BF),
            pltpu.VMEM((512, 256), BF),
            pltpu.VMEM((512, 256), F32),
            grad_shape,
        ],
        [
            stage,
            pltpu.VMEM((3, 544, 1152), BF),
            pltpu.VMEM((3, 1152, 256), BF),
            pltpu.SemaphoreType.DMA((3,)),
        ]
        + grad_scratch(1),
        16,
        5 * unit,
        [VM, HB, VM, VM],
        [VM] * 3 + [HB],
    )(x, in_hbm(taps), bias.reshape(1, 256), out_grad)
    feat0, pg0 = call(
        first_kernel, [pltpu.VMEM((512, 256), BF), pltpu.VMEM((512, 256), BF)], [], 8, unit // 10, [VM] * 3
    )(pre0, prior, out_grad)
    after = passed_along(pg0, -1)
    core = (lax.axis_index("dp") % 2).astype(jnp.int32).reshape(1)
    features, q, dw, early, held = call(
        middle_kernel,
        [
            shape(2, 512, 256),
            pltpu.VMEM((2, 544, 1152), BF),
            pltpu.VMEM((2, 1152, 256), F32),
            pltpu.VMEM((2, 1280, 128), BF),
            grad_shape,
        ],
        [
            stage,
            pltpu.VMEM((2, 544, 1152), BF),
            pltpu.VMEM((3, 1152, 256), BF),
            pltpu.SemaphoreType.DMA((5,)),
        ]
        + grad_scratch(1),
        16,
        6 * unit,
        [SM, VM, HB] + [VM] * 4 + [HB],
        [HB, VM, VM, VM, HB],
        {7: 4},
    )(core, x, in_hbm(taps), pg0, pg1, feat0, feat1, held)
    early_got = lax.ppermute(early[1], AXES, CORE_SWAP)
    late = call(weight_kernel, [pltpu.VMEM((2, 2304, 128), BF)], [], 8, 2 * unit, [SM] + [VM] * 3)(core, q, after, dw)
    late_got = lax.ppermute(late[1], AXES, CORE_SWAP)
    mine = call(join_kernel, [JOINED((3584, 128), BF)], [], 8, unit // 10, [VM] * 4)(late, late_got, early, early_got)
    pieces = spread_over(mine.reshape(TEAM, SHARE, 128))
    clips_grad = call(
        high_kernel, [grad_shape], grad_scratch(2), 8, 4 * unit, [VM] * 3 + [HB], [HB], {3: 0}
    )(taps, pg1, after, held)
    positions = 1024 * lax.axis_size("tm") * lax.axis_size("dp")
    total = jnp.sum(pieces.astype(F32), axis=0)
    total = total + lax.ppermute(total, AXES, ROW_SWAP)
    total = (total * (1.0 / math.sqrt(positions))).astype(BF)
    own = spread_over(jnp.broadcast_to(total[None], (TEAM, SHARE, 128))).reshape(3584, 128)
    weight_grad, bias_grad = finish(core, own)
    features = features.reshape(1, 2, 16, 32, 256)
    return features, clips_grad, weight_grad.reshape(3, 3, 3, 128, 256), bias_grad.reshape(256)


def solution(mesh):
    in_specs = (P("dp", "tm", None, None, None), P(), P(), P("dp", "tm", None, None, None))
    out_specs = (P("dp", "tm", None, None, None), P("dp", "tm", None, None, None), P(), P())
    return jax.shard_map(local, mesh=mesh, in_specs=in_specs, out_specs=out_specs, check_vma=False)
```
